32 devices in a mesh: parts: 2 (over y), blk: 4 (over z), grp: 4 (over x, core).
Axes of the slice: x: 2, y: 2, z: 4, core: 2. Of those that a mesh axis runs over, the one named last changes fastest.
Arguments:
- factors: float32 [64, 4096], P(None, ('parts', 'blk', 'grp')), parts along dimension 1, may hold values from -1 to 1
- tangent: float32 [64, 4096], P(None, ('parts', 'blk', 'grp')), parts along dimension 1, may hold values from -15 to 15
- counts: int32 [4096, 2048], P(('parts', 'blk', 'grp')), parts along dimension 0, may hold values from 0 to 4, as said below
Outputs:
- hess_vec: float32 [64, 4096], P(None, ('parts', 'blk', 'grp')), parts along dimension 1
- residual: float32 [64, 4096], P(None, ('parts', 'blk', 'grp')), parts along dimension 1
- inner: float32 [4], P('parts'), parts along dimension 0
The draws below stay inside these ranges and needn't reach their ends.
There are 2 independent parts, one for each index of `parts`. The reference program is written for one: setup_inputs(seed, part) draws one part's arguments, and reference() takes and returns one part's arrays. A program takes and returns all parts, laid end to end along the dimension named above; each array names one. Nothing has to cross between parts.
Inputs may be any that keep to these rules, and one draw needn't show every extreme that they name: counts is symmetric.
All inputs are finite; a program needn't handle non-finite values.
Results may differ from the reference program's by a relative error of at most 0.0003.
Values sent between devices are 32-bit elements; how exact they have to be, the bound alone decides.
A program may use at most 128 MiB of HBM per device.

```python
import jax
import jax.numpy as jnp
from jax import lax

RANK = 64
ROWS_DEV = 128
NODES = 2048
N_BLK = 4
N_GRP = 4


def draw_tangent(key, part):
    key_base = jax.random.fold_in(key, 11)
    key_jit = jax.random.fold_in(key, 12)
    node = jnp.arange(NODES, dtype=jnp.float32) / NODES
    jitter = jnp.exp(jax.random.uniform(key_jit, (1, NODES), jnp.float32, jnp.log(0.6), jnp.log(1.6)))
    base = jnp.clip(jax.random.normal(key_base, (RANK, NODES), jnp.float32), -4.0, 4.0)
    rise = jnp.exp(jnp.log(3.0) * node)[None, :]
    return 0.25 * base * rise * jitter


def draw_counts(key, part):
    upper = jax.random.randint(jax.random.fold_in(key, 21), (NODES, NODES), 0, 3, dtype=jnp.int32)
    return upper + upper.T


def block_levels(own_key, dims, shards, smallest, high):
    level, own = 1.0, jax.random.fold_in(own_key, 6)
    for dim, blocks in shards:
        steps = jnp.exp(jax.random.uniform(jax.random.fold_in(own, dim), (blocks,), jnp.float32, smallest / len(shards), high / len(shards)))
        level = level * jnp.repeat(steps, dims[dim] // blocks).reshape([-1 if axis == dim else 1 for axis in range(len(dims))])
    return level


def scatter_about(rng, shape, width, bound, cuts=(), kind=jnp.bfloat16):
    drawn = jax.random.normal(rng, shape, jnp.float32) * width
    if len(cuts) > 0:
        drawn = block_levels(rng, shape, cuts, -0.22, 0.18) * drawn
    return jnp.clip(drawn, min=-bound, max=bound).astype(kind)


def setup_inputs(seed: int = 0, part: int = 0) -> dict:
    keys = jax.random.split(jax.random.key(seed), 4)
    own_keys = jax.random.split(jax.random.fold_in(keys[3], part), 4)
    return {
        "factors": scatter_about(own_keys[0], (RANK, NODES), 0.25, 1.0, ((1, 16),), jnp.float32),
        "tangent": draw_tangent(jax.random.fold_in(jax.random.fold_in(keys[3], part), 71), part),
        "counts": draw_counts(jax.random.fold_in(jax.random.fold_in(keys[3], part), 71), part),
    }


def reference(factors, tangent, counts):
    scale = 1.0 / jnp.sqrt(jnp.float32(NODES))
    step = ROWS_DEV * N_GRP
    highest = lax.Precision.HIGHEST
    contract = (((0,), (0,)), ((), ()))
    right = (((1,), (1,)), ((), ()))

    def one_block(index):
        start = (index * step).astype(jnp.int32)
        row_u = lax.dynamic_slice_in_dim(factors, start, step, 1)
        row_v = lax.dynamic_slice_in_dim(tangent, start, step, 1)
        row_c = lax.dynamic_slice_in_dim(counts, start, step, 0).astype(jnp.float32)
        eta = lax.dot_general(row_u, factors, contract, precision=highest)
        deta = lax.dot_general(row_u, tangent, contract, precision=highest) + lax.dot_general(row_v, factors, contract, precision=highest)
        row_ids = start + jnp.arange(step, dtype=jnp.int32)[:, None]
        col_ids = jnp.arange(NODES, dtype=jnp.int32)[None, :]
        keep = row_ids != col_ids
        rate = jnp.where(keep, jnp.exp(eta), jnp.float32(0.0))
        weight = rate * deta
        slack = jnp.where(keep, row_c - rate, jnp.float32(0.0))
        hess_part = lax.dot_general(factors, weight, right, precision=highest)
        resid_part = lax.dot_general(factors, slack - weight, right, precision=highest)
        return (hess_part, resid_part)
    hess_blocks, resid_blocks = lax.map(one_block, jnp.arange(N_BLK, dtype=jnp.int32))
    hess_vec = jnp.transpose(hess_blocks, (1, 0, 2)).reshape(RANK, NODES) * scale
    residual = jnp.transpose(resid_blocks, (1, 0, 2)).reshape(RANK, NODES) * scale
    inner = jnp.stack([jnp.sum(residual * residual), jnp.sum(tangent * hess_vec)])
    return (hess_vec, residual, inner)
```

```python
import functools

import jax
import jax.numpy as jnp
from jax import lax
from jax.experimental import pallas as pl
from jax.experimental.pallas import tpu as pltpu
from jax.sharding import PartitionSpec as P

MESH = pl.DeviceIdType.MESH


def split(x):
    hi = x.astype(jnp.bfloat16)
    lo = (x - hi.astype(jnp.float32)).astype(jnp.bfloat16)
    return hi, lo


def kernel(
    n_blk,
    n_grp,
    f_hbm,
    t_hbm,
    c_hbm,
    h_hbm,
    r_hbm,
    inner_ref,
    slots,
    counts,
    lhs,
    acc,
    h_buf,
    r_buf,
    stats,
    local_sem,
    z_sem,
    x_sem,
    s_sem,
    recv_sem,
    stat_send,
    stat_recv,
):
    n_x = n_grp // 2
    n_dev = n_blk * n_grp
    rank, rows = h_buf.shape
    nodes = counts.shape[1]
    blk = lax.axis_index("blk")
    grp = lax.axis_index("grp")
    x, core = grp // 2, lax.rem(grp, 2)
    me = blk * n_grp + grp
    sibling = 2 * x + 1 - core

    def peer(k):
        there = lax.rem(me + k, n_dev)
        return there, {"blk": there // n_grp, "grp": lax.rem(there, n_grp)}

    load_f = pltpu.make_async_copy(f_hbm, slots.at[me, pl.ds(0, rank)], local_sem.at[0])
    load_t = pltpu.make_async_copy(t_hbm, slots.at[me, pl.ds(rank, rank)], local_sem.at[1])
    load_c = pltpu.make_async_copy(c_hbm, counts, local_sem.at[2])
    load_f.start()
    load_t.start()
    load_c.start()

    barrier = pltpu.get_barrier_semaphore()

    @pl.loop(1, n_dev)
    def _(k):
        pl.semaphore_signal(barrier, inc=1, device_id=peer(k)[1], device_id_type=MESH)

    load_f.wait()
    load_t.wait()
    pl.semaphore_wait(barrier, n_dev - 1)

    def send(slot, b, g, sem):
        return pltpu.make_async_remote_copy(
            src_ref=slots.at[slot],
            dst_ref=slots.at[slot],
            send_sem=sem,
            recv_sem=recv_sem.at[slot],
            device_id={"blk": b, "grp": g},
            device_id_type=MESH,
        )

    def arrived(slot):
        send(slot, blk, sibling, s_sem.at[0]).wait_recv()

    def to_z(k):
        return send(me, lax.rem(blk + k, n_blk), grp, z_sem.at[k])

    def from_z(k):
        return lax.rem(blk + n_blk - k, n_blk)

    def x_at(dx):
        return lax.rem(x + dx, n_x)

    def to_x(k, dx):
        return send(from_z(k) * n_grp + grp, blk, 2 * x_at(dx) + core, x_sem.at[k, dx])

    def to_sibling(k, dx):
        return send(from_z(k) * n_grp + 2 * x_at(dx) + core, blk, sibling, s_sem.at[k * n_x + dx])

    def slot_own_core(k, dx):
        return from_z(k) * n_grp + 2 * x_at(dx) + core

    def slot_sibling(k, dx):
        return from_z(k) * n_grp + 2 * x_at(dx) + 1 - core

    for k in range(1, n_blk):
        to_z(k).start()
    for dx in range(1, n_x):
        to_x(0, dx).start()
    to_sibling(0, 0).start()

    u = slots[me, pl.ds(0, rank), :]
    v = slots[me, pl.ds(rank, rank), :]
    u_hi, u_lo = split(jnp.concatenate([u, jnp.zeros_like(u)], axis=0).T)
    d_hi, d_lo = split(jnp.concatenate([v, u], axis=0).T)
    for i, part in enumerate((u_hi, u_lo, d_hi, d_lo)):
        lhs[pl.ds(i * rows, rows), pl.ds(0, 2 * rank)] = part
        lhs[pl.ds(i * rows, rows), pl.ds(2 * rank, 2 * rank)] = part
    acc[...] = jnp.zeros_like(acc)
    load_c.wait()

    def tile(b, xx):
        pair = b * n_grp + 2 * xx
        width = 2 * rows
        start = pl.multiple_of(pair * rows, width)
        block = jnp.concatenate([slots[pair], slots[pair + 1]], axis=1)
        hi, lo = split(block)
        both = jnp.concatenate([hi, lo], axis=0)
        z = jnp.dot(lhs[...], both, preferred_element_type=jnp.float32)
        eta = z[:rows] + z[rows : 2 * rows]
        deta = z[2 * rows : 3 * rows] + z[3 * rows :]
        col = lax.broadcasted_iota(jnp.int32, (rows, width), 1)
        row = lax.broadcasted_iota(jnp.int32, (rows, width), 0)
        keep = (col - row) != (me - pair) * rows
        rate = jnp.where(keep, jnp.exp(eta), 0.0)
        weight = rate * deta
        c = counts[:, pl.ds(start, width)].astype(jnp.float32)
        slack = jnp.where(keep, c - rate, 0.0)
        w_hi, w_lo = split(weight)
        t_hi, t_lo = split(slack - weight)
        p = jnp.concatenate([w_hi, w_lo, t_hi, t_lo], axis=0)
        uu = jnp.concatenate([hi[:rank], lo[:rank]], axis=0)
        acc[...] += lax.dot_general(
            p, uu, (((1,), (1,)), ((), ())), preferred_element_type=jnp.float32
        )

    def step(k, _):
        @pl.when(k < n_blk)
        def _():
            @pl.when(k > 0)
            def _():
                arrived(slot_own_core(k, 0))
                for dx in range(1, n_x):
                    to_x(k, dx).start()
                to_sibling(k, 0).start()

        @pl.when(jnp.logical_and(k > 0, k <= n_blk))
        def _():
            for dx in range(1, n_x):
                arrived(slot_own_core(k - 1, dx))
                to_sibling(k - 1, dx).start()
            arrived(slot_sibling(k - 1, 0))
            tile(from_z(k - 1), x)

        @pl.when(k > 1)
        def _():
            @pl.loop(1, n_x)
            def _(dx):
                arrived(slot_sibling(k - 2, dx))
                tile(from_z(k - 2), x_at(dx))

        return 0

    lax.fori_loop(0, n_blk + 2, step, 0)

    scale = 1.0 / jnp.sqrt(jnp.float32(nodes))
    h = (acc[pl.ds(0, rows)] + acc[pl.ds(rows, rows)]).T
    r = (acc[pl.ds(2 * rows, rows)] + acc[pl.ds(3 * rows, rows)]).T
    h = (h[:rank] + h[rank:]) * scale
    r = (r[:rank] + r[rank:]) * scale
    h_buf[...] = h
    r_buf[...] = r
    sq = r * r
    curv = slots[me, pl.ds(rank, rank), :] * h
    stats[me, pl.ds(0, 8)] = jnp.sum(sq.reshape(rank // 8, 8, rows), axis=0)
    stats[me, pl.ds(8, 8)] = jnp.sum(curv.reshape(rank // 8, 8, rows), axis=0)

    def to_stat(k):
        return pltpu.make_async_remote_copy(
            src_ref=stats.at[me],
            dst_ref=stats.at[me],
            send_sem=stat_send.at[k],
            recv_sem=stat_recv.at[me],
            device_id=peer(k)[1],
            device_id_type=MESH,
        )

    def stat_arrived(k):
        there = peer(k)[0]
        pltpu.make_async_remote_copy(
            src_ref=stats.at[there],
            dst_ref=stats.at[there],
            send_sem=stat_send.at[0],
            recv_sem=stat_recv.at[there],
            device_id=peer(k)[1],
            device_id_type=MESH,
        ).wait_recv()

    @pl.loop(1, n_dev)
    def _(k):
        to_stat(k).start()

    store_h = pltpu.make_async_copy(h_buf, h_hbm, local_sem.at[0])
    store_r = pltpu.make_async_copy(r_buf, r_hbm, local_sem.at[1])
    store_h.start()
    store_r.start()

    @pl.loop(1, n_blk)
    def _(k):
        to_z(k).wait_send()

    @pl.loop(0, n_blk)
    def _(k):
        for dx in range(n_x):
            if dx > 0:
                to_x(k, dx).wait_send()
            to_sibling(k, dx).wait_send()

    @pl.loop(1, n_dev)
    def _(k):
        stat_arrived(k)

    total = jnp.sum(stats[...], axis=0)
    inner_ref[0] = jnp.sum(total[:8])
    inner_ref[1] = jnp.sum(total[8:])

    @pl.loop(1, n_dev)
    def _(k):
        to_stat(k).wait_send()

    store_h.wait()
    store_r.wait()


def local(n_blk, n_grp, factors, tangent, counts):
    rank, rows = factors.shape
    nodes = counts.shape[1]
    n_x = n_grp // 2
    n_dev = n_blk * n_grp
    anyspace = pl.BlockSpec(memory_space=pl.ANY)
    flat = jax.ShapeDtypeStruct((rank, rows), jnp.float32)
    return pl.pallas_call(
        functools.partial(kernel, n_blk, n_grp),
        out_shape=(flat, flat, jax.ShapeDtypeStruct((2,), jnp.float32)),
        in_specs=[anyspace] * 3,
        out_specs=(anyspace, anyspace, pl.BlockSpec(memory_space=pltpu.SMEM)),
        scratch_shapes=[
            pltpu.VMEM((n_dev, 2 * rank, rows), jnp.float32),
            pltpu.VMEM((rows, nodes), jnp.int32),
            pltpu.VMEM((4 * rows, 4 * rank), jnp.bfloat16),
            pltpu.VMEM((4 * rows, 2 * rank), jnp.float32),
            pltpu.VMEM((rank, rows), jnp.float32),
            pltpu.VMEM((rank, rows), jnp.float32),
            pltpu.VMEM((n_dev, 16, rows), jnp.float32),
            pltpu.SemaphoreType.DMA((3,)),
            pltpu.SemaphoreType.DMA((n_blk,)),
            pltpu.SemaphoreType.DMA((n_blk, n_x)),
            pltpu.SemaphoreType.DMA((n_dev,)),
            pltpu.SemaphoreType.DMA((n_dev,)),
            pltpu.SemaphoreType.DMA((n_dev,)),
            pltpu.SemaphoreType.DMA((n_dev,)),
        ],
        compiler_params=pltpu.CompilerParams(
            collective_id=0, has_side_effects=True, vmem_limit_bytes=64 * 1024 * 1024 - 64 * 1024
        ),
    )(factors, tangent, counts)


def solution(mesh):
    nodes = P(None, ("parts", "blk", "grp"))
    return jax.shard_map(
        functools.partial(local, mesh.shape["blk"], mesh.shape["grp"]),
        mesh=mesh,
        in_specs=(nodes, nodes, P(("parts", "blk", "grp"), None)),
        out_specs=(nodes, nodes, P("parts")),
        check_vma=False,
    )
```

```python
import functools

import jax
import jax.numpy as jnp
from jax import lax
from jax.experimental import pallas as pl
from jax.experimental.pallas import tpu as pltpu
from jax.sharding import PartitionSpec as P

MESH = pl.DeviceIdType.MESH


def split(x):
    hi = x.astype(jnp.bfloat16)
    lo = (x - hi.astype(jnp.float32)).astype(jnp.bfloat16)
    return hi, lo


def kernel(
    n_blk,
    n_grp,
    f_hbm,
    t_hbm,
    c_hbm,
    h_hbm,
    r_hbm,
    inner_ref,
    slots,
    counts,
    lhs,
    acc,
    h_buf,
    r_buf,
    stats,
    local_sem,
    z_sem,
    x_sem,
    s_sem,
    recv_sem,
    stat_send,
    stat_recv,
):
    n_x = n_grp // 2
    n_dev = n_blk * n_grp
    rank, rows = h_buf.shape
    nodes = counts.shape[1]
    blk = lax.axis_index("blk")
    grp = lax.axis_index("grp")
    x, core = grp // 2, lax.rem(grp, 2)
    me = blk * n_grp + grp
    sibling = 2 * x + 1 - core

    def peer(k):
        there = lax.rem(me + k, n_dev)
        return there, {"blk": there // n_grp, "grp": lax.rem(there, n_grp)}

    load_f = pltpu.make_async_copy(f_hbm, slots.at[me, pl.ds(0, rank)], local_sem.at[0])
    load_t = pltpu.make_async_copy(t_hbm, slots.at[me, pl.ds(rank, rank)], local_sem.at[1])
    load_c = pltpu.make_async_copy(c_hbm, counts, local_sem.at[2])
    load_f.start()
    load_t.start()
    load_c.start()

    barrier = pltpu.get_barrier_semaphore()

    @pl.loop(1, n_dev)
    def _(k):
        pl.semaphore_signal(barrier, inc=1, device_id=peer(k)[1], device_id_type=MESH)

    load_f.wait()
    load_t.wait()
    pl.semaphore_wait(barrier, n_dev - 1)

    def send(slot, half, b, g, sem):
        part = slots.at[slot, pl.ds(half * rank, rank)]
        return pltpu.make_async_remote_copy(
            src_ref=part,
            dst_ref=part,
            send_sem=sem,
            recv_sem=recv_sem.at[slot, half],
            device_id={"blk": b, "grp": g},
            device_id_type=MESH,
        )

    def arrived(slot, half):
        send(slot, half, blk, sibling, s_sem.at[0, 0]).wait_recv()

    def x_at(dx):
        return lax.rem(x + dx, n_x)

    def to_z(b, half, there, k):
        return send(b * n_grp + grp, half, there, grp, z_sem.at[k, half])

    def to_x(b, dx, half):
        return send(b * n_grp + grp, half, blk, 2 * x_at(dx) + core, x_sem.at[b, dx, half])

    def to_sibling(b, dx, half):
        slot = b * n_grp + 2 * x_at(dx) + core
        return send(slot, half, blk, sibling, s_sem.at[slot, half])

    def inside(b):
        return jnp.logical_and(b >= 0, b < n_blk)

    for half in range(2):
        for k, there in enumerate((blk - 1, blk + 1)):

            @pl.when(inside(there))
            def _():
                to_z(blk, half, there, blk if k == 0 else n_blk).start()

        for dx in range(1, n_x):
            to_x(blk, dx, half).start()
        to_sibling(blk, 0, half).start()

    u = slots[me, pl.ds(0, rank), :]
    v = slots[me, pl.ds(rank, rank), :]
    u_hi, u_lo = split(jnp.concatenate([u, jnp.zeros_like(u)], axis=0).T)
    d_hi, d_lo = split(jnp.concatenate([v, u], axis=0).T)
    for i, part in enumerate((u_hi, u_lo, d_hi, d_lo)):
        lhs[pl.ds(i * rows, rows), pl.ds(0, 2 * rank)] = part
        lhs[pl.ds(i * rows, rows), pl.ds(2 * rank, 2 * rank)] = part
    acc[...] = jnp.zeros_like(acc)
    load_c.wait()

    def tile(b, xx):
        pair = b * n_grp + 2 * xx
        width = 2 * rows
        start = pl.multiple_of(pair * rows, width)
        block = jnp.concatenate([slots[pair], slots[pair + 1]], axis=1)
        hi, lo = split(block)
        both = jnp.concatenate([hi, lo], axis=0)
        z = jnp.dot(lhs[...], both, preferred_element_type=jnp.float32)
        eta = z[:rows] + z[rows : 2 * rows]
        deta = z[2 * rows : 3 * rows] + z[3 * rows :]
        col = lax.broadcasted_iota(jnp.int32, (rows, width), 1)
        row = lax.broadcasted_iota(jnp.int32, (rows, width), 0)
        keep = (col - row) != (me - pair) * rows
        rate = jnp.where(keep, jnp.exp(eta), 0.0)
        weight = rate * deta
        c = counts[:, pl.ds(start, width)].astype(jnp.float32)
        slack = jnp.where(keep, c - rate, 0.0)
        w_hi, w_lo = split(weight)
        t_hi, t_lo = split(slack - weight)
        p = jnp.concatenate([w_hi, w_lo, t_hi, t_lo], axis=0)
        uu = jnp.concatenate([hi[:rank], lo[:rank]], axis=0)
        acc[...] += lax.dot_general(
            p, uu, (((1,), (1,)), ((), ())), preferred_element_type=jnp.float32
        )

    def step(k, _):
        for half in range(2):
            for side in (-1, 1):
                b = blk + side * k

                @pl.when(jnp.logical_and(k > 0, inside(b)))
                def _():
                    arrived(b * n_grp + grp, half)

                    @pl.when(inside(blk - side))
                    def _():
                        to_z(b, half, blk - side, b).start()

                    for dx in range(1, n_x):
                        to_x(b, dx, half).start()
                    to_sibling(b, 0, half).start()

        for half in range(2):
            for side in (-1, 1):
                b = blk + side * (k - 1)
                first = jnp.logical_or(k > 1, side > 0)

                @pl.when(jnp.logical_and(jnp.logical_and(k > 0, first), inside(b)))
                def _():
                    for dx in range(1, n_x):
                        arrived(b * n_grp + 2 * x_at(dx) + core, half)
                        to_sibling(b, dx, half).start()

        for side in (-1, 1):
            b = blk + side * (k - 1)
            first = jnp.logical_or(k > 1, side > 0)

            @pl.when(jnp.logical_and(jnp.logical_and(k > 0, first), inside(b)))
            def _():
                arrived(b * n_grp + 2 * x + 1 - core, 0)
                arrived(b * n_grp + 2 * x + 1 - core, 1)
                tile(b, x)

        for side in (-1, 1):
            b = blk + side * (k - 2)
            first = jnp.logical_or(k > 2, side > 0)

            @pl.when(jnp.logical_and(jnp.logical_and(k > 1, first), inside(b)))
            def _():
                @pl.loop(1, n_x)
                def _(dx):
                    arrived(b * n_grp + 2 * x_at(dx) + 1 - core, 0)
                    arrived(b * n_grp + 2 * x_at(dx) + 1 - core, 1)
                    tile(b, x_at(dx))

        return 0

    lax.fori_loop(0, n_blk + 2, step, 0)

    scale = 1.0 / jnp.sqrt(jnp.float32(nodes))
    h = (acc[pl.ds(0, rows)] + acc[pl.ds(rows, rows)]).T
    r = (acc[pl.ds(2 * rows, rows)] + acc[pl.ds(3 * rows, rows)]).T
    h = (h[:rank] + h[rank:]) * scale
    r = (r[:rank] + r[rank:]) * scale
    h_buf[...] = h
    r_buf[...] = r
    sq = r * r
    curv = slots[me, pl.ds(rank, rank), :] * h
    sq = jnp.sum(sq.reshape(rank // 8, 8, rows), axis=0)
    curv = jnp.sum(curv.reshape(rank // 8, 8, rows), axis=0)
    stats[me] = jnp.concatenate([sq[:4] + sq[4:], curv[:4] + curv[4:]], axis=0)

    def to_stat(k):
        return pltpu.make_async_remote_copy(
            src_ref=stats.at[me],
            dst_ref=stats.at[me],
            send_sem=stat_send.at[k],
            recv_sem=stat_recv.at[me],
            device_id=peer(k)[1],
            device_id_type=MESH,
        )

    def stat_arrived(k):
        there = peer(k)[0]
        pltpu.make_async_remote_copy(
            src_ref=stats.at[there],
            dst_ref=stats.at[there],
            send_sem=stat_send.at[0],
            recv_sem=stat_recv.at[there],
            device_id=peer(k)[1],
            device_id_type=MESH,
        ).wait_recv()

    for k in range(1, n_dev):
        to_stat(k).start()

    store_h = pltpu.make_async_copy(h_buf, h_hbm, local_sem.at[0])
    store_r = pltpu.make_async_copy(r_buf, r_hbm, local_sem.at[1])
    store_h.start()
    store_r.start()

    for half in range(2):
        for k, there in enumerate((blk - 1, blk + 1)):

            @pl.when(inside(there))
            def _():
                to_z(blk, half, there, blk if k == 0 else n_blk).wait_send()

    @pl.loop(0, n_blk)
    def _(b):
        there = jnp.where(b < blk, blk + 1, blk - 1)

        @pl.when(jnp.logical_and(b != blk, inside(there)))
        def _():
            for half in range(2):
                to_z(b, half, there, b).wait_send()

        for half in range(2):
            for dx in range(n_x):
                if dx > 0:
                    to_x(b, dx, half).wait_send()
                to_sibling(b, dx, half).wait_send()

    for k in range(1, n_dev):
        stat_arrived(k)

    total = jnp.sum(stats[...], axis=0)
    inner_ref[0] = jnp.sum(total[:4])
    inner_ref[1] = jnp.sum(total[4:])

    for k in range(1, n_dev):
        to_stat(k).wait_send()

    store_h.wait()
    store_r.wait()


def local(n_blk, n_grp, factors, tangent, counts):
    rank, rows = factors.shape
    nodes = counts.shape[1]
    n_x = n_grp // 2
    n_dev = n_blk * n_grp
    anyspace = pl.BlockSpec(memory_space=pl.ANY)
    flat = jax.ShapeDtypeStruct((rank, rows), jnp.float32)
    return pl.pallas_call(
        functools.partial(kernel, n_blk, n_grp),
        out_shape=(flat, flat, jax.ShapeDtypeStruct((2,), jnp.float32)),
        in_specs=[anyspace] * 3,
        out_specs=(anyspace, anyspace, pl.BlockSpec(memory_space=pltpu.SMEM)),
        scratch_shapes=[
            pltpu.VMEM((n_dev, 2 * rank, rows), jnp.float32),
            pltpu.VMEM((rows, nodes), jnp.int32),
            pltpu.VMEM((4 * rows, 4 * rank), jnp.bfloat16),
            pltpu.VMEM((4 * rows, 2 * rank), jnp.float32),
            pltpu.VMEM((rank, rows), jnp.float32),
            pltpu.VMEM((rank, rows), jnp.float32),
            pltpu.VMEM((n_dev, 8, rows), jnp.float32),
            pltpu.SemaphoreType.DMA((3,)),
            pltpu.SemaphoreType.DMA((n_blk + 1, 2)),
            pltpu.SemaphoreType.DMA((n_blk, n_x, 2)),
            pltpu.SemaphoreType.DMA((n_dev, 2)),
            pltpu.SemaphoreType.DMA((n_dev, 2)),
            pltpu.SemaphoreType.DMA((n_dev,)),
            pltpu.SemaphoreType.DMA((n_dev,)),
        ],
        compiler_params=pltpu.CompilerParams(
            collective_id=0, has_side_effects=True, vmem_limit_bytes=64 * 1024 * 1024 - 64 * 1024
        ),
    )(factors, tangent, counts)


def solution(mesh):
    nodes = P(None, ("parts", "blk", "grp"))
    return jax.shard_map(
        functools.partial(local, mesh.shape["blk"], mesh.shape["grp"]),
        mesh=mesh,
        in_specs=(nodes, nodes, P(("parts", "blk", "grp"), None)),
        out_specs=(nodes, nodes, P("parts")),
        check_vma=False,
    )
```

```python
import functools

import jax
import jax.numpy as jnp
from jax import lax
from jax.experimental import pallas as pl
from jax.experimental.pallas import tpu as pltpu
from jax.sharding import PartitionSpec as P

MESH = pl.DeviceIdType.MESH


def split(x):
    hi = x.astype(jnp.bfloat16)
    lo = (x - hi.astype(jnp.float32)).astype(jnp.bfloat16)
    return hi, lo


def kernel(
    n_blk,
    n_grp,
    f_hbm,
    t_hbm,
    c_hbm,
    h_hbm,
    r_hbm,
    inner_ref,
    slots,
    counts,
    lhs,
    acc,
    h_buf,
    r_buf,
    stats,
    local_sem,
    z_sem,
    x_sem,
    s_sem,
    recv_sem,
    stat_send,
    stat_recv,
):
    n_x = n_grp // 2
    n_dev = n_blk * n_grp
    rank, rows = h_buf.shape
    nodes = counts.shape[1]
    blk = lax.axis_index("blk")
    grp = lax.axis_index("grp")
    x, core = grp // 2, lax.rem(grp, 2)
    me = blk * n_grp + grp
    sibling = 2 * x + 1 - core

    pairs, pair, odd = n_blk // 2, blk // 2, lax.rem(blk, 2)

    def x_at(dx):
        return lax.rem(x + dx, n_x)

    def target(e):
        return lax.rem(pair + e // 2, pairs) * 2 + lax.rem(odd + e, 2)

    def source(e):
        return lax.rem(pair + pairs - e // 2, pairs) * 2 + lax.rem(odd + e, 2)

    load_f = pltpu.make_async_copy(f_hbm, slots.at[me, pl.ds(0, rank)], local_sem.at[0])
    load_t = pltpu.make_async_copy(t_hbm, slots.at[me, pl.ds(rank, rank)], local_sem.at[1])
    load_c = pltpu.make_async_copy(c_hbm, counts, local_sem.at[2])
    load_f.start()
    load_t.start()
    load_c.start()

    barrier = pltpu.get_barrier_semaphore()

    friends = [(e, 0) for e in range(n_blk - 1, 0, -1)]
    friends += [(e, dx) for e in (1, 0) for dx in range(1, n_x)]
    for e, dx in friends:
        pl.semaphore_signal(
            barrier,
            inc=1,
            device_id={"blk": target(e), "grp": 2 * x_at(dx) + core},
            device_id_type=MESH,
        )
    pl.semaphore_signal(
        barrier, inc=1, device_id={"blk": blk, "grp": sibling}, device_id_type=MESH
    )

    load_f.wait()
    load_t.wait()
    pl.semaphore_wait(barrier, len(friends) + 1)

    def send(slot, b, g, sem):
        return pltpu.make_async_remote_copy(
            src_ref=slots.at[slot],
            dst_ref=slots.at[slot],
            send_sem=sem,
            recv_sem=recv_sem.at[slot],
            device_id={"blk": b, "grp": g},
            device_id_type=MESH,
        )

    def slot_at(e, dx, c):
        return source(e) * n_grp + 2 * x_at(dx) + c

    def arrived(e, dx, c):
        send(slot_at(e, dx, c), blk, sibling, s_sem.at[0]).wait_recv()

    def to_z(e):
        return send(me, target(e), grp, z_sem.at[e])

    def to_x(e, dx):
        there = 2 * x_at(dx) + core
        if isinstance(e, int) and e < 2:
            return send(me, target(e), there, x_sem.at[e, dx])
        return send(slot_at(e, 0, core), blk, there, x_sem.at[e, dx])

    def to_sibling(e, dx):
        return send(slot_at(e, dx, core), blk, sibling, s_sem.at[e * n_x + dx])

    for e in range(2, n_blk):
        to_z(e).start()
    for dx in range(1, n_x):
        to_x(0, dx).start()
    to_z(1).start()
    for dx in range(1, n_x):
        to_x(1, dx).start()
    to_sibling(0, 0).start()

    u = slots[me, pl.ds(0, rank), :]
    v = slots[me, pl.ds(rank, rank), :]
    u_hi, u_lo = split(jnp.concatenate([u, jnp.zeros_like(u)], axis=0).T)
    d_hi, d_lo = split(jnp.concatenate([v, u], axis=0).T)
    for i, part in enumerate((u_hi, u_lo, d_hi, d_lo)):
        lhs[pl.ds(i * rows, rows), pl.ds(0, 2 * rank)] = part
        lhs[pl.ds(i * rows, rows), pl.ds(2 * rank, 2 * rank)] = part
    acc[...] = jnp.zeros_like(acc)
    load_c.wait()

    def tile(b, xx):
        pair = b * n_grp + 2 * xx
        width = 2 * rows
        start = pl.multiple_of(pair * rows, width)
        block = jnp.concatenate([slots[pair], slots[pair + 1]], axis=1)
        hi, lo = split(block)
        both = jnp.concatenate([hi, lo], axis=0)
        z = jnp.dot(lhs[...], both, preferred_element_type=jnp.float32)
        eta = z[:rows] + z[rows : 2 * rows]
        deta = z[2 * rows : 3 * rows] + z[3 * rows :]
        col = lax.broadcasted_iota(jnp.int32, (rows, width), 1)
        row = lax.broadcasted_iota(jnp.int32, (rows, width), 0)
        keep = (col - row) != (me - pair) * rows
        rate = jnp.where(keep, jnp.exp(eta), 0.0)
        weight = rate * deta
        c = counts[:, pl.ds(start, width)].astype(jnp.float32)
        slack = jnp.where(keep, c - rate, 0.0)
        w_hi, w_lo = split(weight)
        t_hi, t_lo = split(slack - weight)
        p = jnp.concatenate([w_hi, w_lo, t_hi, t_lo], axis=0)
        uu = jnp.concatenate([hi[:rank], lo[:rank]], axis=0)
        acc[...] += lax.dot_general(
            p, uu, (((1,), (1,)), ((), ())), preferred_element_type=jnp.float32
        )

    def own_tile(e):
        arrived(e, 0, 1 - core)
        tile(source(e), x)

    def other_tiles(e):
        @pl.loop(1, n_x)
        def _(dx):
            arrived(e, dx, 1 - core)
            tile(source(e), x_at(dx))

    def pass_x(e):
        for dx in range(1, n_x):
            arrived(e, dx, core)
            to_sibling(e, dx).start()

    own_tile(0)
    pass_x(0)
    arrived(1, 0, core)
    to_sibling(1, 0).start()
    pass_x(1)

    @pl.loop(2, n_blk)
    def _(e):
        arrived(e, 0, core)
        for dx in range(1, n_x):
            to_x(e, dx).start()
        to_sibling(e, 0).start()

        @pl.when(e == 2)
        def _():
            other_tiles(0)

    own_tile(1)
    other_tiles(1)

    @pl.loop(2, n_blk)
    def _(e):
        own_tile(e)
        pass_x(e)

    @pl.loop(2, n_blk)
    def _(e):
        other_tiles(e)

    scale = 1.0 / jnp.sqrt(jnp.float32(nodes))
    h = (acc[pl.ds(0, rows)] + acc[pl.ds(rows, rows)]).T
    r = (acc[pl.ds(2 * rows, rows)] + acc[pl.ds(3 * rows, rows)]).T
    h = (h[:rank] + h[rank:]) * scale
    r = (r[:rank] + r[rank:]) * scale
    h_buf[...] = h
    r_buf[...] = r
    sq = r * r
    curv = slots[me, pl.ds(rank, rank), :] * h
    sq = jnp.sum(sq.reshape(rank // 8, 8, rows), axis=0)
    curv = jnp.sum(curv.reshape(rank // 8, 8, rows), axis=0)
    stats[me] = jnp.concatenate([sq[:4] + sq[4:], curv[:4] + curv[4:]], axis=0)

    others = [
        (e, dx, c) for e in range(n_blk - 1, -1, -1) for dx in range(n_x - 1, -1, -1) for c in range(2)
    ][:-1]

    def stat(slot, b, g, k):
        return pltpu.make_async_remote_copy(
            src_ref=stats.at[slot],
            dst_ref=stats.at[slot],
            send_sem=stat_send.at[k],
            recv_sem=stat_recv.at[slot],
            device_id={"blk": b, "grp": g},
            device_id_type=MESH,
        )

    def to_stat(k):
        e, dx, c = others[k]
        return stat(me, target(e), 2 * x_at(dx) + lax.rem(core + 1 - c, 2), k)

    def stat_arrived(k):
        e, dx, c = others[k]
        stat(slot_at(e, dx, lax.rem(core + 1 - c, 2)), blk, sibling, 0).wait_recv()

    for k in range(n_dev - 1):
        to_stat(k).start()

    store_h = pltpu.make_async_copy(h_buf, h_hbm, local_sem.at[0])
    store_r = pltpu.make_async_copy(r_buf, r_hbm, local_sem.at[1])
    store_h.start()
    store_r.start()

    for e in range(1, n_blk):
        to_z(e).wait_send()
    for e in range(n_blk):
        for dx in range(n_x):
            if dx > 0:
                to_x(e, dx).wait_send()
            to_sibling(e, dx).wait_send()

    for k in range(n_dev - 1):
        stat_arrived(k)

    total = jnp.sum(stats[...], axis=0)
    inner_ref[0] = jnp.sum(total[:4])
    inner_ref[1] = jnp.sum(total[4:])

    for k in range(n_dev - 1):
        to_stat(k).wait_send()

    store_h.wait()
    store_r.wait()


def local(n_blk, n_grp, factors, tangent, counts):
    rank, rows = factors.shape
    nodes = counts.shape[1]
    n_x = n_grp // 2
    n_dev = n_blk * n_grp
    anyspace = pl.BlockSpec(memory_space=pl.ANY)
    flat = jax.ShapeDtypeStruct((rank, rows), jnp.float32)
    return pl.pallas_call(
        functools.partial(kernel, n_blk, n_grp),
        out_shape=(flat, flat, jax.ShapeDtypeStruct((2,), jnp.float32)),
        in_specs=[anyspace] * 3,
        out_specs=(anyspace, anyspace, pl.BlockSpec(memory_space=pltpu.SMEM)),
        scratch_shapes=[
            pltpu.VMEM((n_dev, 2 * rank, rows), jnp.float32),
            pltpu.VMEM((rows, nodes), jnp.int32),
            pltpu.VMEM((4 * rows, 4 * rank), jnp.bfloat16),
            pltpu.VMEM((4 * rows, 2 * rank), jnp.float32),
            pltpu.VMEM((rank, rows), jnp.float32),
            pltpu.VMEM((rank, rows), jnp.float32),
            pltpu.VMEM((n_dev, 8, rows), jnp.float32),
            pltpu.SemaphoreType.DMA((3,)),
            pltpu.SemaphoreType.DMA((n_blk,)),
            pltpu.SemaphoreType.DMA((n_blk, n_x)),
            pltpu.SemaphoreType.DMA((n_blk * n_x,)),
            pltpu.SemaphoreType.DMA((n_dev,)),
            pltpu.SemaphoreType.DMA((n_dev,)),
            pltpu.SemaphoreType.DMA((n_dev,)),
        ],
        compiler_params=pltpu.CompilerParams(
            collective_id=0, has_side_effects=True, vmem_limit_bytes=64 * 1024 * 1024 - 64 * 1024
        ),
    )(factors, tangent, counts)


def solution(mesh):
    nodes = P(None, ("parts", "blk", "grp"))
    return jax.shard_map(
        functools.partial(local, mesh.shape["blk"], mesh.shape["grp"]),
        mesh=mesh,
        in_specs=(nodes, nodes, P(("parts", "blk", "grp"), None)),
        out_specs=(nodes, nodes, P("parts")),
        check_vma=False,
    )
```

```python
import functools

import jax
import jax.numpy as jnp
from jax import lax
from jax.experimental import pallas as pl
from jax.experimental.pallas import tpu as pltpu
from jax.sharding import PartitionSpec as P

MESH = pl.DeviceIdType.MESH


def split(x):
    hi = x.astype(jnp.bfloat16)
    lo = (x - hi.astype(jnp.float32)).astype(jnp.bfloat16)
    return hi, lo


def kernel(
    n_blk,
    n_grp,
    f_hbm,
    t_hbm,
    c_hbm,
    out_hbm,
    slots,
    counts,
    lhs,
    acc,
    out_buf,
    stats,
    local_sem,
    z_sem,
    x_sem,
    s_sem,
    recv_sem,
    stat_send,
    stat_recv,
):
    n_x = n_grp // 2
    n_dev = n_blk * n_grp
    rank, rows = f_hbm.shape
    nodes = counts.shape[1]
    blk = lax.axis_index("blk")
    grp = lax.axis_index("grp")
    x, core = grp // 2, lax.rem(grp, 2)
    me = blk * n_grp + grp
    sibling = 2 * x + 1 - core

    pairs, pair, odd = n_blk // 2, blk // 2, lax.rem(blk, 2)

    def x_at(dx):
        return lax.rem(x + dx, n_x)

    def target(e):
        return lax.rem(pair + e // 2, pairs) * 2 + lax.rem(odd + e, 2)

    def source(e):
        return lax.rem(pair + pairs - e // 2, pairs) * 2 + lax.rem(odd + e, 2)

    load_f = pltpu.make_async_copy(f_hbm, slots.at[me, pl.ds(0, rank)], local_sem.at[0])
    load_t = pltpu.make_async_copy(t_hbm, slots.at[me, pl.ds(rank, rank)], local_sem.at[1])
    load_c = pltpu.make_async_copy(c_hbm, counts, local_sem.at[2])
    load_f.start()
    load_t.start()
    load_c.start()

    barrier = pltpu.get_barrier_semaphore()

    friends = [(e, 0) for e in range(2, n_blk, 2)]
    friends += [(e, dx) for e in (1, 0) for dx in range(1 - e, n_x)]
    for e, dx in friends:
        pl.semaphore_signal(
            barrier,
            inc=1,
            device_id={"blk": target(e), "grp": 2 * x_at(dx) + core},
            device_id_type=MESH,
        )
    pl.semaphore_signal(
        barrier, inc=1, device_id={"blk": blk, "grp": sibling}, device_id_type=MESH
    )

    load_f.wait()
    load_t.wait()
    pl.semaphore_wait(barrier, len(friends) + 1)

    def send(slot, b, g, sem):
        return pltpu.make_async_remote_copy(
            src_ref=slots.at[slot],
            dst_ref=slots.at[slot],
            send_sem=sem,
            recv_sem=recv_sem.at[slot],
            device_id={"blk": b, "grp": g},
            device_id_type=MESH,
        )

    def slot_at(e, dx, c):
        return source(e) * n_grp + 2 * x_at(dx) + c

    def arrived(e, dx, c):
        send(slot_at(e, dx, c), blk, sibling, s_sem.at[0]).wait_recv()

    def to_z(e):
        return send(me, target(e), grp, z_sem.at[e])

    def to_x(e, dx):
        return send(me, target(e), 2 * x_at(dx) + core, x_sem.at[e, dx])

    def relay(e):
        slot = slot_at(e, 0, core)
        return [
            send(slot, b, 2 * x_at(dx) + core, x_sem.at[e, dx + n_x * k])
            for k, b in ((1, target(1)), (0, blk))
            for dx in range(n_x - 1, -k, -1)
        ]

    def to_sibling(e, dx):
        return send(slot_at(e, dx, core), blk, sibling, s_sem.at[e * n_x + dx])

    for e in range(2, n_blk, 2):
        to_z(e).start()
    for dx in range(1, n_x):
        to_x(0, dx).start()
    to_z(1).start()
    for dx in range(1, n_x):
        to_x(1, dx).start()
    to_sibling(0, 0).start()

    u = slots[me, pl.ds(0, rank), :]
    v = slots[me, pl.ds(rank, rank), :]
    u_hi, u_lo = split(jnp.concatenate([u, jnp.zeros_like(u)], axis=0).T)
    d_hi, d_lo = split(jnp.concatenate([v, u], axis=0).T)
    for i, part in enumerate((u_hi, u_lo, d_hi, d_lo)):
        lhs[pl.ds(i * rows, rows), pl.ds(0, 2 * rank)] = part
        lhs[pl.ds(i * rows, rows), pl.ds(2 * rank, 2 * rank)] = part
    acc[...] = jnp.zeros_like(acc)
    load_c.wait()

    def tile(b, xx):
        pair = b * n_grp + 2 * xx
        width = 2 * rows
        start = pl.multiple_of(pair * rows, width)
        block = jnp.concatenate([slots[pair], slots[pair + 1]], axis=1)
        hi, lo = split(block)
        both = jnp.concatenate([hi, lo], axis=0)
        z = jnp.dot(lhs[...], both, preferred_element_type=jnp.float32)
        eta = z[:rows] + z[rows : 2 * rows]
        deta = z[2 * rows : 3 * rows] + z[3 * rows :]
        col = lax.broadcasted_iota(jnp.int32, (rows, width), 1)
        row = lax.broadcasted_iota(jnp.int32, (rows, width), 0)
        keep = (col - row) != (me - pair) * rows
        rate = jnp.where(keep, jnp.exp(eta), 0.0)
        weight = rate * deta
        c = counts[:, pl.ds(start, width)].astype(jnp.float32)
        slack = jnp.where(keep, c - rate, 0.0)
        w_hi, w_lo = split(weight)
        t_hi, t_lo = split(slack - weight)
        p = jnp.concatenate([w_hi, w_lo, t_hi, t_lo], axis=0)
        uu = jnp.concatenate([hi[:rank], lo[:rank]], axis=0)
        acc[...] += lax.dot_general(
            p, uu, (((1,), (1,)), ((), ())), preferred_element_type=jnp.float32
        )

    def own_tile(e):
        arrived(e, 0, 1 - core)
        tile(source(e), x)

    def other_tiles(e):
        @pl.loop(1, n_x)
        def _(dx):
            arrived(e, dx, 1 - core)
            tile(source(e), x_at(dx))

    def pass_x(e):
        for dx in range(1, n_x):
            arrived(e, dx, core)
            to_sibling(e, dx).start()

    own_tile(0)
    pass_x(0)
    arrived(1, 0, core)
    to_sibling(1, 0).start()
    pass_x(1)

    @pl.loop(1, pairs)
    def _(m):
        arrived(2 * m, 0, core)
        for copy in relay(2 * m):
            copy.start()
        to_sibling(2 * m, 0).start()

    other_tiles(0)
    own_tile(1)
    other_tiles(1)

    @pl.loop(1, pairs)
    def _(m):
        own_tile(2 * m)
        pass_x(2 * m)
        arrived(2 * m + 1, 0, core)
        to_sibling(2 * m + 1, 0).start()
        pass_x(2 * m + 1)

    @pl.loop(1, pairs)
    def _(m):
        other_tiles(2 * m)
        own_tile(2 * m + 1)
        other_tiles(2 * m + 1)

    scale = 1.0 / jnp.sqrt(jnp.float32(nodes))
    h = (acc[pl.ds(0, rows)] + acc[pl.ds(rows, rows)]).T
    r = (acc[pl.ds(2 * rows, rows)] + acc[pl.ds(3 * rows, rows)]).T
    h = (h[:rank] + h[rank:]) * scale
    r = (r[:rank] + r[rank:]) * scale
    out_buf[pl.ds(0, rank)] = h
    out_buf[pl.ds(rank, rank)] = r
    sq = r * r
    curv = slots[me, pl.ds(rank, rank), :] * h
    sq = jnp.sum(sq.reshape(rank // 8, 8, rows), axis=0)
    curv = jnp.sum(curv.reshape(rank // 8, 8, rows), axis=0)
    stats[me] = jnp.concatenate([sq[:4] + sq[4:], curv[:4] + curv[4:]], axis=0)

    others = [
        (e, dx, c) for e in range(n_blk - 1, -1, -1) for dx in range(n_x - 1, -1, -1) for c in range(2)
    ][:-1]

    def stat(slot, b, g, k):
        return pltpu.make_async_remote_copy(
            src_ref=stats.at[slot],
            dst_ref=stats.at[slot],
            send_sem=stat_send.at[k],
            recv_sem=stat_recv.at[slot],
            device_id={"blk": b, "grp": g},
            device_id_type=MESH,
        )

    def to_stat(k):
        e, dx, c = others[k]
        return stat(me, target(e), 2 * x_at(dx) + lax.rem(core + 1 - c, 2), k)

    def stat_arrived(k):
        e, dx, c = others[k]
        stat(slot_at(e, dx, lax.rem(core + 1 - c, 2)), blk, sibling, 0).wait_recv()

    for k in range(n_dev - 1):
        to_stat(k).start()

    top, end = pl.ds(0, 2 * rank), pl.ds(2 * rank, 8)
    store = pltpu.make_async_copy(out_buf.at[top], out_hbm.at[top], local_sem.at[0])
    store_sums = pltpu.make_async_copy(out_buf.at[end], out_hbm.at[end], local_sem.at[1])
    store.start()

    to_z(1).wait_send()
    for e in range(2, n_blk, 2):
        to_z(e).wait_send()
        for copy in relay(e):
            copy.wait_send()
    for e in range(2):
        for dx in range(1, n_x):
            to_x(e, dx).wait_send()
    for e in range(n_blk):
        for dx in range(n_x):
            to_sibling(e, dx).wait_send()

    for k in range(n_dev - 1):
        stat_arrived(k)

    total = jnp.sum(stats[...], axis=0)
    sums = jnp.where(
        lax.broadcasted_iota(jnp.int32, (8, rows), 1) == 0, jnp.sum(total[:4]), jnp.sum(total[4:])
    )
    out_buf[end] = sums
    store_sums.start()

    for k in range(n_dev - 1):
        to_stat(k).wait_send()

    store.wait()
    store_sums.wait()


def unpack(packed, h_ref, r_ref, inner_ref):
    rank = h_ref.shape[0]
    h_ref[...] = packed[pl.ds(0, rank)]
    r_ref[...] = packed[pl.ds(rank, rank)]
    inner_ref[0] = packed[2 * rank, 0]
    inner_ref[1] = packed[2 * rank, 1]


def local(n_blk, n_grp, factors, tangent, counts):
    rank, rows = factors.shape
    nodes = counts.shape[1]
    n_x = n_grp // 2
    n_dev = n_blk * n_grp
    anyspace = pl.BlockSpec(memory_space=pl.ANY)
    packed = pl.pallas_call(
        functools.partial(kernel, n_blk, n_grp),
        out_shape=jax.ShapeDtypeStruct((2 * rank + 8, rows), jnp.float32),
        in_specs=[anyspace] * 3,
        out_specs=anyspace,
        scratch_shapes=[
            pltpu.VMEM((n_dev, 2 * rank, rows), jnp.float32),
            pltpu.VMEM((rows, nodes), jnp.int32),
            pltpu.VMEM((4 * rows, 4 * rank), jnp.bfloat16),
            pltpu.VMEM((4 * rows, 2 * rank), jnp.float32),
            pltpu.VMEM((2 * rank + 8, rows), jnp.float32),
            pltpu.VMEM((n_dev, 8, rows), jnp.float32),
            pltpu.SemaphoreType.DMA((3,)),
            pltpu.SemaphoreType.DMA((n_blk,)),
            pltpu.SemaphoreType.DMA((n_blk, 2 * n_x)),
            pltpu.SemaphoreType.DMA((n_blk * n_x,)),
            pltpu.SemaphoreType.DMA((n_dev,)),
            pltpu.SemaphoreType.DMA((n_dev,)),
            pltpu.SemaphoreType.DMA((n_dev,)),
        ],
        compiler_params=pltpu.CompilerParams(
            collective_id=0, has_side_effects=True, vmem_limit_bytes=64 * 1024 * 1024 - 64 * 1024
        ),
    )(factors, tangent, counts)
    flat = jax.ShapeDtypeStruct((rank, rows), jnp.float32)
    return pl.pallas_call(
        unpack,
        out_shape=(flat, flat, jax.ShapeDtypeStruct((2,), jnp.float32)),
        in_specs=[pl.BlockSpec(memory_space=pltpu.VMEM)],
        out_specs=(pl.BlockSpec(memory_space=pltpu.VMEM), pl.BlockSpec(memory_space=pltpu.VMEM), pl.BlockSpec(memory_space=pltpu.SMEM)),
    )(packed)


def solution(mesh):
    nodes = P(None, ("parts", "blk", "grp"))
    return jax.shard_map(
        functools.partial(local, mesh.shape["blk"], mesh.shape["grp"]),
        mesh=mesh,
        in_specs=(nodes, nodes, P(("parts", "blk", "grp"), None)),
        out_specs=(nodes, nodes, P("parts")),
        check_vma=False,
    )
```

```python
import functools

import jax
import jax.numpy as jnp
from jax import lax
from jax.experimental import pallas as pl
from jax.experimental.pallas import tpu as pltpu
from jax.sharding import PartitionSpec as P

MESH = pl.DeviceIdType.MESH


def split(x):
    hi = x.astype(jnp.bfloat16)
    lo = (x - hi.astype(jnp.float32)).astype(jnp.bfloat16)
    return hi, lo


def kernel(
    n_blk,
    n_grp,
    f_hbm,
    t_hbm,
    c_hbm,
    out_hbm,
    slots,
    counts,
    lhs,
    acc,
    out_buf,
    stats,
    local_sem,
    z_sem,
    x_sem,
    s_sem,
    recv_sem,
    stat_send,
    stat_recv,
):
    n_x = n_grp // 2
    n_dev = n_blk * n_grp
    rank, rows = f_hbm.shape
    nodes = counts.shape[1]
    blk = lax.axis_index("blk")
    grp = lax.axis_index("grp")
    x, core = grp // 2, lax.rem(grp, 2)
    me = blk * n_grp + grp
    sibling = 2 * x + 1 - core

    pairs, pair, odd = n_blk // 2, blk // 2, lax.rem(blk, 2)

    def x_at(dx):
        return lax.rem(x + dx, n_x)

    def target(e):
        return lax.rem(pair + e // 2, pairs) * 2 + lax.rem(odd + e, 2)

    def source(e):
        return lax.rem(pair + pairs - e // 2, pairs) * 2 + lax.rem(odd + e, 2)

    load_f = pltpu.make_async_copy(f_hbm, slots.at[me, pl.ds(0, rank)], local_sem.at[0])
    load_t = pltpu.make_async_copy(t_hbm, slots.at[me, pl.ds(rank, rank)], local_sem.at[1])
    load_c = pltpu.make_async_copy(c_hbm, counts, local_sem.at[2])
    load_f.start()
    load_t.start()
    load_c.start()

    barrier = pltpu.get_barrier_semaphore()

    friends = [(e, 0) for e in range(2, n_blk, 2)]
    friends += [(e, dx) for e in (1, 0) for dx in range(1 - e, n_x)]
    for e, dx in friends:
        pl.semaphore_signal(
            barrier,
            inc=1,
            device_id={"blk": target(e), "grp": 2 * x_at(dx) + core},
            device_id_type=MESH,
        )
    pl.semaphore_signal(
        barrier, inc=1, device_id={"blk": blk, "grp": sibling}, device_id_type=MESH
    )

    load_f.wait()
    load_t.wait()
    pl.semaphore_wait(barrier, len(friends) + 1)

    def send(slot, b, g, sem):
        return pltpu.make_async_remote_copy(
            src_ref=slots.at[slot],
            dst_ref=slots.at[slot],
            send_sem=sem,
            recv_sem=recv_sem.at[slot],
            device_id={"blk": b, "grp": g},
            device_id_type=MESH,
        )

    def slot_at(e, dx, c):
        return source(e) * n_grp + 2 * x_at(dx) + c

    def arrived(e, dx, c):
        send(slot_at(e, dx, c), blk, sibling, s_sem.at[0]).wait_recv()

    def to_z(e):
        return send(me, target(e), grp, z_sem.at[e])

    def to_x(e, dx):
        return send(me, target(e), 2 * x_at(dx) + core, x_sem.at[e, dx])

    def relay(e):
        slot = slot_at(e, 0, core)
        return [
            send(slot, b, 2 * x_at(dx) + core, x_sem.at[e, dx + n_x * k])
            for k, b in ((1, target(1)), (0, blk))
            for dx in range(n_x - 1, -k, -1)
        ]

    def to_sibling(e, dx):
        return send(slot_at(e, dx, core), blk, sibling, s_sem.at[e * n_x + dx])

    for e in range(2, n_blk, 2):
        to_z(e).start()
    for dx in range(1, n_x):
        to_x(0, dx).start()
    to_z(1).start()
    for dx in range(1, n_x):
        to_x(1, dx).start()
    to_sibling(0, 0).start()

    u = slots[me, pl.ds(0, rank), :]
    v = slots[me, pl.ds(rank, rank), :]
    u_hi, u_lo = split(jnp.concatenate([u, jnp.zeros_like(u)], axis=0).T)
    d_hi, d_lo = split(jnp.concatenate([v, u], axis=0).T)
    for i, part in enumerate((u_hi, u_lo, d_hi, d_lo)):
        lhs[pl.ds(i * rows, rows), pl.ds(0, 2 * rank)] = part
        lhs[pl.ds(i * rows, rows), pl.ds(2 * rank, 2 * rank)] = part
    acc[...] = jnp.zeros_like(acc)
    load_c.wait()

    def tile(b, xx):
        pair = b * n_grp + 2 * xx
        width = 2 * rows
        start = pl.multiple_of(pair * rows, width)
        block = jnp.concatenate([slots[pair], slots[pair + 1]], axis=1)
        hi, lo = split(block)
        both = jnp.concatenate([hi, lo], axis=0)
        z = jnp.dot(lhs[...], both, preferred_element_type=jnp.float32)
        eta = z[:rows] + z[rows : 2 * rows]
        deta = z[2 * rows : 3 * rows] + z[3 * rows :]
        col = lax.broadcasted_iota(jnp.int32, (rows, width), 1)
        row = lax.broadcasted_iota(jnp.int32, (rows, width), 0)
        keep = (col - row) != (me - pair) * rows
        rate = jnp.where(keep, jnp.exp(eta), 0.0)
        weight = rate * deta
        c = counts[:, pl.ds(start, width)].astype(jnp.float32)
        slack = jnp.where(keep, c - rate, 0.0)
        w_hi, w_lo = split(weight)
        t_hi, t_lo = split(slack - weight)
        p = jnp.concatenate([w_hi, w_lo, t_hi, t_lo], axis=0)
        uu = jnp.concatenate([hi[:rank], lo[:rank]], axis=0)
        acc[...] += lax.dot_general(
            p, uu, (((1,), (1,)), ((), ())), preferred_element_type=jnp.float32
        )

    def own_tile(e):
        arrived(e, 0, 1 - core)
        tile(source(e), x)

    def other_tiles(e):
        @pl.loop(1, n_x)
        def _(dx):
            arrived(e, dx, 1 - core)
            tile(source(e), x_at(dx))

    def pass_x(e):
        for dx in range(1, n_x):
            arrived(e, dx, core)
            to_sibling(e, dx).start()

    own_tile(0)
    pass_x(0)
    @pl.loop(1, pairs)
    def _(m):
        arrived(2 * m, 0, core)
        for copy in relay(2 * m):
            copy.start()
        to_sibling(2 * m, 0).start()

    arrived(1, 0, core)
    to_sibling(1, 0).start()
    pass_x(1)

    other_tiles(0)
    own_tile(1)
    other_tiles(1)

    @pl.loop(1, pairs)
    def _(m):
        own_tile(2 * m)
        pass_x(2 * m)
        arrived(2 * m + 1, 0, core)
        to_sibling(2 * m + 1, 0).start()
        pass_x(2 * m + 1)

    @pl.loop(1, pairs)
    def _(m):
        other_tiles(2 * m)
        own_tile(2 * m + 1)
        other_tiles(2 * m + 1)

    scale = 1.0 / jnp.sqrt(jnp.float32(nodes))
    h = (acc[pl.ds(0, rows)] + acc[pl.ds(rows, rows)]).T
    r = (acc[pl.ds(2 * rows, rows)] + acc[pl.ds(3 * rows, rows)]).T
    h = (h[:rank] + h[rank:]) * scale
    r = (r[:rank] + r[rank:]) * scale
    out_buf[pl.ds(0, rank)] = h
    out_buf[pl.ds(rank, rank)] = r
    sq = r * r
    curv = slots[me, pl.ds(rank, rank), :] * h
    sq = jnp.sum(sq.reshape(rank // 8, 8, rows), axis=0)
    curv = jnp.sum(curv.reshape(rank // 8, 8, rows), axis=0)
    stats[me] = jnp.concatenate([sq[:4] + sq[4:], curv[:4] + curv[4:]], axis=0)

    others = [
        (e, dx, c) for e in range(n_blk - 1, -1, -1) for dx in range(n_x - 1, -1, -1) for c in range(2)
    ][:-1]

    def stat(slot, b, g, k):
        return pltpu.make_async_remote_copy(
            src_ref=stats.at[slot],
            dst_ref=stats.at[slot],
            send_sem=stat_send.at[k],
            recv_sem=stat_recv.at[slot],
            device_id={"blk": b, "grp": g},
            device_id_type=MESH,
        )

    def to_stat(k):
        e, dx, c = others[k]
        return stat(me, target(e), 2 * x_at(dx) + lax.rem(core + 1 - c, 2), k)

    def stat_arrived(k):
        e, dx, c = others[k]
        stat(slot_at(e, dx, lax.rem(core + 1 - c, 2)), blk, sibling, 0).wait_recv()

    for k in range(n_dev - 1):
        to_stat(k).start()

    top, end = pl.ds(0, 2 * rank), pl.ds(2 * rank, 8)
    store = pltpu.make_async_copy(out_buf.at[top], out_hbm.at[top], local_sem.at[0])
    store_sums = pltpu.make_async_copy(out_buf.at[end], out_hbm.at[end], local_sem.at[1])
    store.start()

    to_z(1).wait_send()
    for e in range(2, n_blk, 2):
        to_z(e).wait_send()
        for copy in relay(e):
            copy.wait_send()
    for e in range(2):
        for dx in range(1, n_x):
            to_x(e, dx).wait_send()
    for e in range(n_blk):
        for dx in range(n_x):
            to_sibling(e, dx).wait_send()

    for k in range(n_dev - 1):
        stat_arrived(k)

    total = jnp.sum(stats[...], axis=0)
    sums = jnp.where(
        lax.broadcasted_iota(jnp.int32, (8, rows), 1) == 0, jnp.sum(total[:4]), jnp.sum(total[4:])
    )
    out_buf[end] = sums
    store_sums.start()

    for k in range(n_dev - 1):
        to_stat(k).wait_send()

    store.wait()
    store_sums.wait()


def unpack(packed, h_ref, r_ref, inner_ref):
    rank = h_ref.shape[0]
    h_ref[...] = packed[pl.ds(0, rank)]
    r_ref[...] = packed[pl.ds(rank, rank)]
    inner_ref[0] = packed[2 * rank, 0]
    inner_ref[1] = packed[2 * rank, 1]


def local(n_blk, n_grp, factors, tangent, counts):
    rank, rows = factors.shape
    nodes = counts.shape[1]
    n_x = n_grp // 2
    n_dev = n_blk * n_grp
    anyspace = pl.BlockSpec(memory_space=pl.ANY)
    packed = pl.pallas_call(
        functools.partial(kernel, n_blk, n_grp),
        out_shape=jax.ShapeDtypeStruct((2 * rank + 8, rows), jnp.float32),
        in_specs=[anyspace] * 3,
        out_specs=anyspace,
        scratch_shapes=[
            pltpu.VMEM((n_dev, 2 * rank, rows), jnp.float32),
            pltpu.VMEM((rows, nodes), jnp.int32),
            pltpu.VMEM((4 * rows, 4 * rank), jnp.bfloat16),
            pltpu.VMEM((4 * rows, 2 * rank), jnp.float32),
            pltpu.VMEM((2 * rank + 8, rows), jnp.float32),
            pltpu.VMEM((n_dev, 8, rows), jnp.float32),
            pltpu.SemaphoreType.DMA((3,)),
            pltpu.SemaphoreType.DMA((n_blk,)),
            pltpu.SemaphoreType.DMA((n_blk, 2 * n_x)),
            pltpu.SemaphoreType.DMA((n_blk * n_x,)),
            pltpu.SemaphoreType.DMA((n_dev,)),
            pltpu.SemaphoreType.DMA((n_dev,)),
            pltpu.SemaphoreType.DMA((n_dev,)),
        ],
        compiler_params=pltpu.CompilerParams(
            collective_id=0, has_side_effects=True, vmem_limit_bytes=64 * 1024 * 1024 - 64 * 1024
        ),
    )(factors, tangent, counts)
    flat = jax.ShapeDtypeStruct((rank, rows), jnp.float32)
    return pl.pallas_call(
        unpack,
        out_shape=(flat, flat, jax.ShapeDtypeStruct((2,), jnp.float32)),
        in_specs=[pl.BlockSpec(memory_space=pltpu.VMEM)],
        out_specs=(pl.BlockSpec(memory_space=pltpu.VMEM), pl.BlockSpec(memory_space=pltpu.VMEM), pl.BlockSpec(memory_space=pltpu.SMEM)),
    )(packed)


def solution(mesh):
    nodes = P(None, ("parts", "blk", "grp"))
    return jax.shard_map(
        functools.partial(local, mesh.shape["blk"], mesh.shape["grp"]),
        mesh=mesh,
        in_specs=(nodes, nodes, P(("parts", "blk", "grp"), None)),
        out_specs=(nodes, nodes, P("parts")),
        check_vma=False,
    )
```

```python
import functools

import jax
import jax.numpy as jnp
from jax import lax
from jax.experimental import pallas as pl
from jax.experimental.pallas import tpu as pltpu
from jax.sharding import PartitionSpec as P

MESH = pl.DeviceIdType.MESH


def split(x):
    hi = x.astype(jnp.bfloat16)
    lo = (x - hi.astype(jnp.float32)).astype(jnp.bfloat16)
    return hi, lo


def kernel(
    n_blk,
    n_grp,
    f_hbm,
    t_hbm,
    c_hbm,
    out_hbm,
    slots,
    counts,
    lhs,
    acc,
    out_buf,
    stats,
    local_sem,
    z_sem,
    x_sem,
    s_sem,
    recv_sem,
    stat_send,
    stat_recv,
):
    n_x = n_grp // 2
    n_dev = n_blk * n_grp
    rank, rows = f_hbm.shape
    nodes = counts.shape[1]
    blk = lax.axis_index("blk")
    grp = lax.axis_index("grp")
    x, core = grp // 2, lax.rem(grp, 2)
    me = blk * n_grp + grp
    sibling = 2 * x + 1 - core

    pairs, pair, odd = n_blk // 2, blk // 2, lax.rem(blk, 2)

    def x_at(dx):
        return lax.rem(x + dx, n_x)

    def target(e):
        return lax.rem(pair + e // 2, pairs) * 2 + lax.rem(odd + e, 2)

    def source(e):
        return lax.rem(pair + pairs - e // 2, pairs) * 2 + lax.rem(odd + e, 2)

    load_f = pltpu.make_async_copy(f_hbm, slots.at[me, pl.ds(0, rank)], local_sem.at[0])
    load_t = pltpu.make_async_copy(t_hbm, slots.at[me, pl.ds(rank, rank)], local_sem.at[1])
    load_c = pltpu.make_async_copy(c_hbm, counts, local_sem.at[2])
    load_f.start()
    load_t.start()
    load_c.start()

    barrier = pltpu.get_barrier_semaphore()

    friends = [(e, 0) for e in range(2, n_blk, 2)]
    friends += [(e, dx) for e in (1, 0) for dx in range(1 - e, n_x)]
    for e, dx in friends:
        pl.semaphore_signal(
            barrier,
            inc=1,
            device_id={"blk": target(e), "grp": 2 * x_at(dx) + core},
            device_id_type=MESH,
        )
    pl.semaphore_signal(
        barrier, inc=1, device_id={"blk": blk, "grp": sibling}, device_id_type=MESH
    )

    load_f.wait()
    load_t.wait()
    pl.semaphore_wait(barrier, len(friends) + 1)

    def send(slot, b, g, sem):
        return pltpu.make_async_remote_copy(
            src_ref=slots.at[slot],
            dst_ref=slots.at[slot],
            send_sem=sem,
            recv_sem=recv_sem.at[slot],
            device_id={"blk": b, "grp": g},
            device_id_type=MESH,
        )

    def slot_at(e, dx, c):
        return source(e) * n_grp + 2 * x_at(dx) + c

    def arrived(e, dx, c):
        send(slot_at(e, dx, c), blk, sibling, s_sem.at[0]).wait_recv()

    def to_z(e):
        return send(me, target(e), grp, z_sem.at[e])

    def to_x(e, dx):
        return send(me, target(e), 2 * x_at(dx) + core, x_sem.at[e, dx])

    def relay(e):
        slot = slot_at(e, 0, core)
        return [
            send(slot, b, 2 * x_at(dx) + core, x_sem.at[e, dx + n_x * k])
            for k, b in ((1, target(1)), (0, blk))
            for dx in range(n_x - 1, -k, -1)
        ]

    def to_sibling(e, dx):
        return send(slot_at(e, dx, core), blk, sibling, s_sem.at[e * n_x + dx])

    for e in range(2, n_blk, 2):
        to_z(e).start()
    for dx in range(1, n_x):
        to_x(0, dx).start()
    to_z(1).start()
    for dx in range(1, n_x):
        to_x(1, dx).start()
    to_sibling(0, 0).start()

    u = slots[me, pl.ds(0, rank), :]
    v = slots[me, pl.ds(rank, rank), :]
    u_hi, u_lo = split(jnp.concatenate([u, jnp.zeros_like(u)], axis=0).T)
    d_hi, d_lo = split(jnp.concatenate([v, u], axis=0).T)
    for i, part in enumerate((u_hi, u_lo, d_hi, d_lo)):
        lhs[pl.ds(i * rows, rows), pl.ds(0, 2 * rank)] = part
        lhs[pl.ds(i * rows, rows), pl.ds(2 * rank, 2 * rank)] = part
    acc[...] = jnp.zeros_like(acc)
    load_c.wait()

    def tile(b, xx):
        pair = b * n_grp + 2 * xx
        width = 2 * rows
        start = pl.multiple_of(pair * rows, width)
        block = jnp.concatenate([slots[pair], slots[pair + 1]], axis=1)
        hi, lo = split(block)
        both = jnp.concatenate([hi, lo], axis=0)
        z = jnp.dot(lhs[...], both, preferred_element_type=jnp.float32)
        eta = z[:rows] + z[rows : 2 * rows]
        deta = z[2 * rows : 3 * rows] + z[3 * rows :]
        col = lax.broadcasted_iota(jnp.int32, (rows, width), 1)
        row = lax.broadcasted_iota(jnp.int32, (rows, width), 0)
        keep = (col - row) != (me - pair) * rows
        rate = jnp.where(keep, jnp.exp(eta), 0.0)
        weight = rate * deta
        c = counts[:, pl.ds(start, width)].astype(jnp.float32)
        slack = jnp.where(keep, c - rate, 0.0)
        w_hi, w_lo = split(weight)
        t_hi, t_lo = split(slack - weight)
        p = jnp.concatenate([w_hi, w_lo, t_hi, t_lo], axis=0)
        uu = jnp.concatenate([hi[:rank], lo[:rank]], axis=0)
        acc[...] += lax.dot_general(
            p, uu, (((1,), (1,)), ((), ())), preferred_element_type=jnp.float32
        )

    def own_tile(e):
        arrived(e, 0, 1 - core)
        tile(source(e), x)

    def other_tiles(e):
        @pl.loop(1, n_x)
        def _(dx):
            arrived(e, dx, 1 - core)
            tile(source(e), x_at(dx))

    def pass_x(e):
        for dx in range(1, n_x):
            arrived(e, dx, core)
            to_sibling(e, dx).start()

    own_tile(0)
    pass_x(0)
    @pl.loop(1, pairs)
    def _(m):
        arrived(2 * m, 0, core)
        for copy in relay(2 * m):
            copy.start()
        to_sibling(2 * m, 0).start()

    arrived(1, 0, core)
    to_sibling(1, 0).start()
    pass_x(1)

    other_tiles(0)
    own_tile(1)

    @pl.loop(1, pairs)
    def _(m):
        pass_x(2 * m)
        arrived(2 * m + 1, 0, core)
        to_sibling(2 * m + 1, 0).start()
        pass_x(2 * m + 1)

    other_tiles(1)

    @pl.loop(1, pairs)
    def _(m):
        own_tile(2 * m)
        other_tiles(2 * m)
        own_tile(2 * m + 1)
        other_tiles(2 * m + 1)

    scale = 1.0 / jnp.sqrt(jnp.float32(nodes))
    h = (acc[pl.ds(0, rows)] + acc[pl.ds(rows, rows)]).T
    r = (acc[pl.ds(2 * rows, rows)] + acc[pl.ds(3 * rows, rows)]).T
    h = (h[:rank] + h[rank:]) * scale
    r = (r[:rank] + r[rank:]) * scale
    out_buf[pl.ds(0, rank)] = h
    out_buf[pl.ds(rank, rank)] = r
    sq = r * r
    curv = slots[me, pl.ds(rank, rank), :] * h
    sq = jnp.sum(sq.reshape(rank // 8, 8, rows), axis=0)
    curv = jnp.sum(curv.reshape(rank // 8, 8, rows), axis=0)
    stats[me] = jnp.concatenate([sq[:4] + sq[4:], curv[:4] + curv[4:]], axis=0)

    others = [
        (e, dx, c) for e in range(n_blk - 1, -1, -1) for dx in range(n_x - 1, -1, -1) for c in range(2)
    ][:-1]

    def stat(slot, b, g, k):
        return pltpu.make_async_remote_copy(
            src_ref=stats.at[slot],
            dst_ref=stats.at[slot],
            send_sem=stat_send.at[k],
            recv_sem=stat_recv.at[slot],
            device_id={"blk": b, "grp": g},
            device_id_type=MESH,
        )

    def to_stat(k):
        e, dx, c = others[k]
        return stat(me, target(e), 2 * x_at(dx) + lax.rem(core + 1 - c, 2), k)

    def stat_arrived(k):
        e, dx, c = others[k]
        stat(slot_at(e, dx, lax.rem(core + 1 - c, 2)), blk, sibling, 0).wait_recv()

    for k in range(n_dev - 1):
        to_stat(k).start()

    top, end = pl.ds(0, 2 * rank), pl.ds(2 * rank, 8)
    store = pltpu.make_async_copy(out_buf.at[top], out_hbm.at[top], local_sem.at[0])
    store_sums = pltpu.make_async_copy(out_buf.at[end], out_hbm.at[end], local_sem.at[1])
    store.start()

    to_z(1).wait_send()
    for e in range(2, n_blk, 2):
        to_z(e).wait_send()
        for copy in relay(e):
            copy.wait_send()
    for e in range(2):
        for dx in range(1, n_x):
            to_x(e, dx).wait_send()
    for e in range(n_blk):
        for dx in range(n_x):
            to_sibling(e, dx).wait_send()

    for k in range(n_dev - 1):
        stat_arrived(k)

    total = jnp.sum(stats[...], axis=0)
    sums = jnp.where(
        lax.broadcasted_iota(jnp.int32, (8, rows), 1) == 0, jnp.sum(total[:4]), jnp.sum(total[4:])
    )
    out_buf[end] = sums
    store_sums.start()

    for k in range(n_dev - 1):
        to_stat(k).wait_send()

    store.wait()
    store_sums.wait()


def unpack(packed, h_ref, r_ref, inner_ref):
    rank = h_ref.shape[0]
    h_ref[...] = packed[pl.ds(0, rank)]
    r_ref[...] = packed[pl.ds(rank, rank)]
    inner_ref[0] = packed[2 * rank, 0]
    inner_ref[1] = packed[2 * rank, 1]


def local(n_blk, n_grp, factors, tangent, counts):
    rank, rows = factors.shape
    nodes = counts.shape[1]
    n_x = n_grp // 2
    n_dev = n_blk * n_grp
    anyspace = pl.BlockSpec(memory_space=pl.ANY)
    packed = pl.pallas_call(
        functools.partial(kernel, n_blk, n_grp),
        out_shape=jax.ShapeDtypeStruct((2 * rank + 8, rows), jnp.float32),
        in_specs=[anyspace] * 3,
        out_specs=anyspace,
        scratch_shapes=[
            pltpu.VMEM((n_dev, 2 * rank, rows), jnp.float32),
            pltpu.VMEM((rows, nodes), jnp.int32),
            pltpu.VMEM((4 * rows, 4 * rank), jnp.bfloat16),
            pltpu.VMEM((4 * rows, 2 * rank), jnp.float32),
            pltpu.VMEM((2 * rank + 8, rows), jnp.float32),
            pltpu.VMEM((n_dev, 8, rows), jnp.float32),
            pltpu.SemaphoreType.DMA((3,)),
            pltpu.SemaphoreType.DMA((n_blk,)),
            pltpu.SemaphoreType.DMA((n_blk, 2 * n_x)),
            pltpu.SemaphoreType.DMA((n_blk * n_x,)),
            pltpu.SemaphoreType.DMA((n_dev,)),
            pltpu.SemaphoreType.DMA((n_dev,)),
            pltpu.SemaphoreType.DMA((n_dev,)),
        ],
        compiler_params=pltpu.CompilerParams(
            collective_id=0, has_side_effects=True, vmem_limit_bytes=64 * 1024 * 1024 - 64 * 1024
        ),
    )(factors, tangent, counts)
    flat = jax.ShapeDtypeStruct((rank, rows), jnp.float32)
    return pl.pallas_call(
        unpack,
        out_shape=(flat, flat, jax.ShapeDtypeStruct((2,), jnp.float32)),
        in_specs=[pl.BlockSpec(memory_space=pltpu.VMEM)],
        out_specs=(pl.BlockSpec(memory_space=pltpu.VMEM), pl.BlockSpec(memory_space=pltpu.VMEM), pl.BlockSpec(memory_space=pltpu.SMEM)),
    )(packed)


def solution(mesh):
    nodes = P(None, ("parts", "blk", "grp"))
    return jax.shard_map(
        functools.partial(local, mesh.shape["blk"], mesh.shape["grp"]),
        mesh=mesh,
        in_specs=(nodes, nodes, P(("parts", "blk", "grp"), None)),
        out_specs=(nodes, nodes, P("parts")),
        check_vma=False,
    )
```
